32 devices in a mesh: azi: 8 (over z, y), wall: 4 (over x, core).
Axes of the slice: x: 2, y: 2, z: 4, core: 2. Of those that a mesh axis runs over, the one named last changes fastest.
Arguments:
- state: float32 [5, 32, 128, 128], P(None, 'azi', 'wall'), may hold values from -6 to 6
- flux_azi: float32 [5, 5], replicated, may hold values from -2.5 to 2.5
- flux_wall: float32 [5, 5], replicated, may hold values from -2.5 to 2.5
- to_wall: float32 [5, 5], replicated, may hold values from -2.5 to 2.5
- mix_char: float32 [5, 5], replicated, may hold values from -2.5 to 2.5
- from_azi: float32 [5, 5], replicated, may hold values from -2.5 to 2.5
- speed_azi: float32 [5, 32], P(None, 'azi'), may hold values from -1 to 1
- speed_wall: float32 [5, 128], P(None, 'wall'), may hold values from -1 to 1
- visc_azi: float32 [5], replicated, may hold values from 2048 to 16384
- visc_wall: float32 [5], replicated, may hold values from 2048 to 16384
Outputs:
- increment: float32 [5, 32, 128, 128], P(None, 'azi', 'wall')
The draws below stay inside these ranges and needn't reach their ends.
All inputs are finite; a program needn't handle non-finite values.
Results may differ from the reference program's by a relative error of at most 0.0009.
Values sent between devices are 32-bit elements; how exact they have to be, the bound alone decides.
A program may use at most 128 MiB of HBM per device.

```python
import math
import jax
import jax.numpy as jnp
from jax import lax

NVAR = 5
NL = 128
NJ = 32
NK = 128


def level_of(rng, shape, pieces, low, top_value):
    gain = 1.0
    for position, parts in pieces:
        heights = jax.random.uniform(jax.random.fold_in(jax.random.fold_in(rng, 6), position), (parts,), jnp.float32, low / len(pieces), top_value / len(pieces))
        gain = gain * jnp.repeat(jnp.exp(heights), shape[position] // parts).reshape((-1,) + (1,) * (len(shape) - 1 - position))
    return gain


def gaussian(own_key, dims, scale, bound, split=(), kind=jnp.bfloat16):
    entries = jax.random.normal(own_key, dims, jnp.float32) * scale
    if len(split) > 0:
        entries = level_of(own_key, dims, split, -0.22, 0.18) * entries
    return jnp.clip(entries, min=-bound, max=bound).astype(kind)


def setup_inputs(seed: int = 0) -> dict:
    arg_keys = jax.random.split(jax.random.key(seed), 11)
    return {
        "state": gaussian(arg_keys[0], (NVAR, NJ, NK, NL), 1.0, 6.0, ((1, 8), (2, 4)), jnp.float32),
        "flux_azi": gaussian(arg_keys[1], (NVAR, NVAR), NVAR ** -0.5, 2.5, (), jnp.float32),
        "flux_wall": gaussian(arg_keys[2], (NVAR, NVAR), NVAR ** -0.5, 2.5, (), jnp.float32),
        "to_wall": gaussian(arg_keys[3], (NVAR, NVAR), NVAR ** -0.5, 2.5, (), jnp.float32),
        "mix_char": gaussian(arg_keys[4], (NVAR, NVAR), NVAR ** -0.5, 2.5, (), jnp.float32),
        "from_azi": gaussian(arg_keys[5], (NVAR, NVAR), NVAR ** -0.5, 2.5, (), jnp.float32),
        "speed_azi": jnp.clip(jax.random.uniform(arg_keys[6], (NVAR, NJ), jnp.float32, -1.0, 1.0) * level_of(arg_keys[6], (NVAR, NJ), ((1, 8),), -0.4, 0.0), -1.0, 1.0),
        "speed_wall": jnp.clip(jax.random.uniform(arg_keys[7], (NVAR, NK), jnp.float32, -1.0, 1.0) * level_of(arg_keys[7], (NVAR, NK), ((1, 4),), -0.4, 0.0), -1.0, 1.0),
        "visc_azi": jnp.clip(jnp.exp(jax.random.uniform(arg_keys[8], (NVAR,), jnp.float32, math.log(2048.0), math.log(16384.0))), 2048.0, 16384.0),
        "visc_wall": jnp.clip(jnp.exp(jax.random.uniform(arg_keys[9], (NVAR,), jnp.float32, math.log(2048.0), math.log(16384.0))), 2048.0, 16384.0),
    }


time_step = 4096.0
smooth_explicit = 0.02
smooth_implicit = 0.04
highest = lax.Precision.HIGHEST

def mixing(matrix, field):
    return jnp.einsum('ab,bjkl->ajkl', matrix, field, precision=highest)

def residual(padded_azi, padded_wall, flux_azi, flux_wall):
    azi_flux = mixing(flux_azi, padded_azi[:, 1:-1])
    wall_flux = mixing(flux_wall, padded_wall[:, :, 1:-1])
    central = 0.5 * (azi_flux[:, 2:] - azi_flux[:, :-2]) + 0.5 * (wall_flux[:, :, 2:] - wall_flux[:, :, :-2])
    fourth = padded_azi[:, 4:] - 4.0 * padded_azi[:, 3:-1] + 6.0 * padded_azi[:, 2:-2] - 4.0 * padded_azi[:, 1:-3] + padded_azi[:, :-4]
    fourth = fourth + padded_wall[:, :, 4:] - 4.0 * padded_wall[:, :, 3:-1] + 6.0 * padded_wall[:, :, 2:-2] - 4.0 * padded_wall[:, :, 1:-3] + padded_wall[:, :, :-4]
    return -time_step * (central + smooth_explicit * fourth)

def coefficients(speed, visc):
    viscous = visc[:, None]
    below = -0.5 * time_step * speed - viscous - 4.0 * smooth_implicit
    above = 0.5 * time_step * speed - viscous - 4.0 * smooth_implicit
    centre = 1.0 + 2.0 * viscous + 6.0 * smooth_implicit
    return (below, above, centre)

def wall_matrices(speed, visc):
    below, above, centre = coefficients(speed, visc)
    extent = speed.shape[1]

    def shifted(offset):
        return jnp.eye(extent, k=offset, dtype=jnp.float32)
    return centre[:, :, None] * shifted(0) + below[:, :, None] * shifted(-1) + above[:, :, None] * shifted(1) + smooth_implicit * (shifted(2) + shifted(-2))

def cycle_matrices(speed, visc):
    below, above, centre = coefficients(speed, visc)
    extent = speed.shape[1]
    identity = jnp.eye(extent, dtype=jnp.float32)

    def shifted(offset):
        return jnp.roll(identity, offset, axis=1)
    return centre[:, :, None] * identity + below[:, :, None] * shifted(-1) + above[:, :, None] * shifted(1) + smooth_implicit * (shifted(2) + shifted(-2))

def reference(state, flux_azi, flux_wall, to_wall, mix_char, from_azi, speed_azi, speed_wall, visc_azi, visc_wall):
    padded_azi = jnp.concatenate([state[:, -2:], state, state[:, :2]], axis=1)
    padded_wall = jnp.pad(state, ((0, 0), (0, 0), (2, 2), (0, 0)))
    explicit = residual(padded_azi, padded_wall, flux_azi, flux_wall)
    char_wall = mixing(to_wall, explicit)
    cycle_count = state.shape[1]
    wall_count = state.shape[2]
    span_cells = state.shape[3]

    def wall_solve(operands):
        matrix, field = operands
        flat = jnp.transpose(field, (1, 0, 2)).reshape(wall_count, cycle_count * span_cells)
        solved = jnp.linalg.solve(matrix, flat)
        return jnp.transpose(solved.reshape(wall_count, cycle_count, span_cells), (1, 0, 2))
    wall_result = lax.map(wall_solve, (wall_matrices(speed_wall, visc_wall), char_wall))
    cycle_input = mixing(mix_char, wall_result)

    def cycle_solve(operands):
        matrix, field = operands
        flat = field.reshape(cycle_count, wall_count * span_cells)
        return jnp.linalg.solve(matrix, flat).reshape(cycle_count, wall_count, span_cells)
    cycle_result = lax.map(cycle_solve, (cycle_matrices(speed_azi, visc_azi), cycle_input))
    return mixing(from_azi, cycle_result)
```

```python
import functools

import jax
import jax.numpy as jnp
from jax import lax
from jax.experimental import pallas as pl
from jax.experimental.pallas import tpu as pltpu
from jax.sharding import PartitionSpec as P

time_step = 4096.0
smooth_explicit = 0.02
smooth_implicit = 0.04
highest = lax.Precision.HIGHEST


def padded(value, sides, width, wrap):
    for axis, dim in sides:
        size, length = (lax.axis_size(axis), value.shape[dim])
        up = [(i, (i + 1) % size) for i in range(size if wrap else size - 1)]
        down = [(j, i) for i, j in up]
        last = lax.slice_in_dim(value, length - width, length, axis=dim)
        initial = lax.slice_in_dim(value, 0, width, axis=dim)
        before = lax.ppermute(last, axis, up)
        after = lax.ppermute(initial, axis, down)
        value = jnp.concatenate([before, value, after], axis=dim)
    return value


def from_behind(value, axis, by):
    size = lax.axis_size(axis)
    pairs = [(i, i + by) for i in range(size) if 0 <= i + by < size]
    return lax.ppermute(value, axis, pairs)


def from_behind_2(block, axis, distance):
    devices = range(lax.axis_size(axis))
    route = [((i - distance) % len(devices), i) for i in devices]
    return lax.ppermute(block, axis, route)


def mixing(matrix, field):
    return jnp.einsum("ab,bjkl->ajkl", matrix, field, precision=highest)


def residual(padded_azi, padded_wall, flux_azi, flux_wall):
    azi_flux = mixing(flux_azi, padded_azi[:, 1:-1])
    wall_flux = mixing(flux_wall, padded_wall[:, :, 1:-1])
    central = 0.5 * (azi_flux[:, 2:] - azi_flux[:, :-2]) + 0.5 * (
        wall_flux[:, :, 2:] - wall_flux[:, :, :-2]
    )
    fourth = (
        padded_azi[:, 4:]
        - 4.0 * padded_azi[:, 3:-1]
        + 6.0 * padded_azi[:, 2:-2]
        - 4.0 * padded_azi[:, 1:-3]
        + padded_azi[:, :-4]
    )
    fourth = (
        fourth
        + padded_wall[:, :, 4:]
        - 4.0 * padded_wall[:, :, 3:-1]
        + 6.0 * padded_wall[:, :, 2:-2]
        - 4.0 * padded_wall[:, :, 1:-3]
        + padded_wall[:, :, :-4]
    )
    return -time_step * (central + smooth_explicit * fourth)


def coefficients(speed, visc):
    viscous = visc[:, None]
    below = -0.5 * time_step * speed - viscous - 4.0 * smooth_implicit
    above = 0.5 * time_step * speed - viscous - 4.0 * smooth_implicit
    centre = 1.0 + 2.0 * viscous + 6.0 * smooth_implicit
    return (below, above, centre)


def invert(matrices):
    extent = matrices.shape[-1]
    last_axis = matrices.ndim - 1
    identity = jnp.broadcast_to(jnp.eye(extent, dtype=matrices.dtype), matrices.shape)
    marks = lax.broadcasted_iota(jnp.int32, (extent, 1), 0)

    def eliminate(turn, running):
        working, inverse = running
        pivot_row = lax.dynamic_index_in_dim(working, turn, last_axis - 1, keepdims=False)
        inverse_row = lax.dynamic_index_in_dim(inverse, turn, last_axis - 1, keepdims=False)
        column = lax.dynamic_index_in_dim(working, turn, last_axis, keepdims=True)
        pivot = lax.dynamic_index_in_dim(pivot_row, turn, last_axis - 1, keepdims=True)
        pivot_row = pivot_row / pivot
        inverse_row = inverse_row / pivot
        working = working - column * pivot_row[..., None, :]
        inverse = inverse - column * inverse_row[..., None, :]
        on_row = marks == turn
        working = jnp.where(on_row, pivot_row[..., None, :], working)
        inverse = jnp.where(on_row, inverse_row[..., None, :], inverse)
        return (working, inverse)

    return lax.fori_loop(0, extent, eliminate, (matrices, identity))[1]


def two_by_two(first, second, third, fourth):
    return jnp.stack([jnp.stack([first, second], -1), jnp.stack([third, fourth], -1)], -2)


def invert_two(blocks):
    first = blocks[..., 0, 0]
    second = blocks[..., 0, 1]
    third = blocks[..., 1, 0]
    fourth = blocks[..., 1, 1]
    determinant = first * fourth - second * third
    return two_by_two(
        fourth / determinant, -second / determinant, -third / determinant, first / determinant
    )


def block_product(first, second):
    return jnp.einsum("cmab,cmbd->cmad", first, second, precision=highest)


def block_apply(blocks, field):
    return jnp.einsum("cmab,cmbkl->cmakl", blocks, field, precision=highest)


def apply_four(matrix, field):
    return jnp.einsum("cqr,cjrl->cjql", matrix, field, precision=highest)


def product_four(first, second):
    return jnp.einsum("cab,cbd->cad", first, second, precision=highest)


def cyclic_levels(speeds, visc):
    below, above, centre = coefficients(speeds, visc)
    below_even = below[:, 0::2]
    below_odd = below[:, 1::2]
    above_even = above[:, 0::2]
    above_odd = above[:, 1::2]
    edge_value = jnp.full_like(below_even, smooth_implicit)
    nought = jnp.zeros_like(below_even)
    middle_diag = jnp.broadcast_to(centre, below_even.shape)
    behind_block = two_by_two(edge_value, below_even, nought, edge_value)
    middle = two_by_two(middle_diag, above_even, below_odd, middle_diag)
    ahead_block = two_by_two(edge_value, nought, above_odd, edge_value)
    blocks = below_even.shape[1]
    stride = 1
    levels = []
    while stride < blocks:
        weight_before = -block_product(behind_block, invert_two(jnp.roll(middle, stride, 1)))
        weight_after = -block_product(ahead_block, invert_two(jnp.roll(middle, -stride, 1)))
        middle = (
            middle
            + block_product(weight_before, jnp.roll(ahead_block, stride, 1))
            + block_product(weight_after, jnp.roll(behind_block, -stride, 1))
        )
        behind_block = block_product(weight_before, jnp.roll(behind_block, stride, 1))
        ahead_block = block_product(weight_after, jnp.roll(ahead_block, -stride, 1))
        levels.append((stride, weight_before, weight_after))
        stride = stride * 2
    return (levels, invert_two(behind_block + middle + ahead_block))


def per_device(
    state,
    flux_azi,
    flux_wall,
    to_wall,
    mix_char,
    from_azi,
    speed_azi,
    speed_wall,
    visc_azi,
    visc_wall,
):
    padded_azi = padded(state, (("azi", 1),), 2, True)
    padded_wall = padded(state, (("wall", 2),), 2, False)
    explicit = residual(padded_azi, padded_wall, flux_azi, flux_wall)
    char_wall = mixing(to_wall, explicit)
    variables = state.shape[0]
    cycle_cells = state.shape[1]
    wall_depth = state.shape[2]
    span_cells = state.shape[3]
    below, above, centre = coefficients(speed_wall, visc_wall)

    def shifted(offset):
        return jnp.eye(wall_depth, k=offset, dtype=jnp.float32)

    wall_band = (
        centre[:, :, None] * shifted(0)
        + below[:, :, None] * shifted(-1)
        + above[:, :, None] * shifted(1)
        + smooth_implicit * (shifted(2) + shifted(-2))
    )
    local_inverse = invert(wall_band)
    solved = jnp.einsum("ckm,cjml->cjkl", local_inverse, char_wall, precision=highest)
    edge_value = jnp.full_like(below[:, 0], smooth_implicit)
    nought = jnp.zeros_like(edge_value)
    spike_low = jnp.einsum(
        "cka,cab->ckb",
        local_inverse[:, :, 0:2],
        two_by_two(edge_value, below[:, 0], nought, edge_value),
        precision=highest,
    )
    spike_high = jnp.einsum(
        "cka,cab->ckb",
        local_inverse[:, :, wall_depth - 2 :],
        two_by_two(edge_value, nought, above[:, wall_depth - 1], edge_value),
        precision=highest,
    )
    padding = jnp.zeros((variables, 4, 2), jnp.float32)
    ends_low = jnp.concatenate([spike_low[:, 0:2], spike_low[:, wall_depth - 2 :]], 1)
    ends_high = jnp.concatenate([spike_high[:, 0:2], spike_high[:, wall_depth - 2 :]], 1)
    coupling_prev = jnp.concatenate([padding, ends_low], 2)
    coupling_next = jnp.concatenate([ends_high, padding], 2)
    interface = jnp.concatenate([solved[:, :, 0:2], solved[:, :, wall_depth - 2 :]], 2)
    wall_place = lax.axis_index("wall")
    wall_count = lax.axis_size("wall")
    every_prev, every_next = (
        lax.all_gather(coupling_prev, "wall", axis=1, tiled=True),
        lax.all_gather(coupling_next, "wall", axis=1, tiled=True),
    )
    carried = jnp.zeros((variables, 4, 4), jnp.float32)
    identity = jnp.broadcast_to(jnp.eye(4, dtype=jnp.float32), (variables, 4, 4))
    inverses = []
    forwards = []
    for member in range(wall_count):
        pivot_block = identity - product_four(every_prev[:, 4 * member : 4 * member + 4], carried)
        pivot_inverse = invert(pivot_block)
        carried = product_four(pivot_inverse, every_next[:, 4 * member : 4 * member + 4])
        inverses.append(pivot_inverse)
        forwards.append(carried)
    own_inverse = lax.dynamic_index_in_dim(jnp.stack(inverses), wall_place, 0, keepdims=False)
    own_forward = lax.dynamic_index_in_dim(jnp.stack(forwards), wall_place, 0, keepdims=False)
    partial_values = jnp.zeros_like(interface)
    for turn in range(wall_count):
        arrived = from_behind(partial_values, "wall", 1)
        fresh = apply_four(own_inverse, interface - apply_four(coupling_prev, arrived))
        partial_values = jnp.where(wall_place == turn, fresh, partial_values)
    end_values = jnp.zeros_like(interface)
    ahead = jnp.zeros((variables, cycle_cells, 2, span_cells), jnp.float32)
    for turn in reversed(range(wall_count)):
        arrived = from_behind(end_values, "wall", -1)
        fresh = partial_values - apply_four(own_forward, arrived)
        end_values = jnp.where(wall_place == turn, fresh, end_values)
        ahead = jnp.where(wall_place == turn, arrived[:, :, 0:2], ahead)
    behind = from_behind(end_values, "wall", 1)[:, :, 2:4]
    wall_result = (
        solved
        - jnp.einsum("cka,cjal->cjkl", spike_low, behind, precision=highest)
        - jnp.einsum("cka,cjal->cjkl", spike_high, ahead, precision=highest)
    )
    cycle_input = mixing(mix_char, wall_result)
    speeds = lax.all_gather(speed_azi, "azi", axis=1, tiled=True)
    levels, closing = cyclic_levels(speeds, visc_azi)
    half_cells = cycle_cells // 2
    cycle_place = lax.axis_index("azi")

    def own_rows(blocks):
        return lax.dynamic_slice_in_dim(blocks, cycle_place * half_cells, half_cells, 1)

    right_side = cycle_input.reshape(variables, half_cells, 2, wall_depth, span_cells)
    for stride, weight_before, weight_after in levels:
        device_hop = max(1, stride // half_cells)
        reach = min(stride, half_cells)
        from_before = from_behind_2(right_side[:, half_cells - reach :], "azi", device_hop)
        from_after = from_behind_2(right_side[:, :reach], "azi", -device_hop)
        rows_minus = jnp.concatenate([from_before, right_side[:, : half_cells - reach]], 1)
        rows_plus = jnp.concatenate([right_side[:, reach:], from_after], 1)
        right_side = (
            right_side
            + block_apply(own_rows(weight_before), rows_minus)
            + block_apply(own_rows(weight_after), rows_plus)
        )
    cycle_result = block_apply(own_rows(closing), right_side).reshape(
        variables, cycle_cells, wall_depth, span_cells
    )
    return mixing(from_azi, cycle_result)


MESH = pl.DeviceIdType.MESH


def band(speed, visc):
    below = -0.5 * time_step * speed - visc - 4.0 * smooth_implicit
    above = 0.5 * time_step * speed - visc - 4.0 * smooth_implicit
    centre = 1.0 + 2.0 * visc + 6.0 * smooth_implicit
    both = below + above
    part = both - below
    lost = (below - (both - part)) + (above - part)
    total = (centre + both) + lost + 2.0 * smooth_implicit
    return below, above, total


def mix(matrix_ref, fields):
    result = []
    for a in range(len(fields)):
        value = matrix_ref[a, 0] * fields[0]
        for b in range(1, len(fields)):
            value = value + matrix_ref[a, b] * fields[b]
        result.append(value)
    return result


def wall_inverse(speeds_ref, visc, wide_ref, alpha_ref, beta_ref, inverse_ref):
    walls, variables, part = speeds_ref.shape
    cells = walls * part
    lanes = wide_ref.shape[-1]
    for w in range(walls):
        block = speeds_ref[w]
        for k in range(part):
            wide_ref[w * part + k] = jnp.broadcast_to(block[:, k : k + 1], (variables, lanes))
    lane = lax.broadcasted_iota(jnp.int32, (variables, lanes), 1)
    both = lane + lax.broadcasted_iota(jnp.int32, (variables, lanes), 0)
    zero = jnp.where(both < 0, 1.0, 0.0)
    one = jnp.where(both < 0, 0.0, 1.0)

    def forward(k, carry):
        alpha1, beta1, gamma1, sum1, alpha2, beta2, gamma2, sum2 = carry
        below, above, total = band(wide_ref[k], visc)
        lower = below - smooth_implicit * alpha2
        upper = above - lower * beta1
        total = (total - smooth_implicit * sum2) - lower * sum1
        pivot = total - upper - smooth_implicit
        inverse = 1.0 / pivot
        right = jnp.where(lane == k, 1.0, 0.0) - smooth_implicit * gamma2 - lower * gamma1
        alpha = upper * inverse
        beta = smooth_implicit * inverse
        gamma = right * inverse
        alpha_ref[k] = alpha
        beta_ref[k] = beta
        inverse_ref[pl.ds(pl.multiple_of(k * 8, 8), variables), :] = gamma
        return (alpha, beta, gamma, total * inverse, alpha1, beta1, gamma1, sum1)

    lax.fori_loop(0, cells, forward, (zero, zero, zero, one, zero, zero, zero, one), unroll=2)

    def backward(turn, carry):
        x1, x2 = carry
        k = cells - 1 - turn
        rows = pl.ds(pl.multiple_of(k * 8, 8), variables)
        x = (inverse_ref[rows, :] - beta_ref[k] * x2) - alpha_ref[k] * x1
        inverse_ref[rows, :] = x
        return (x, x1)

    lax.fori_loop(0, cells, backward, (zero, zero), unroll=2)


def cycle_inverse(speeds_ref, visc, span, inverse_ref):
    azis, variables, part = speeds_ref.shape
    cells = azis * part
    lanes = inverse_ref.shape[-1]
    lane = lax.broadcasted_iota(jnp.int32, (variables, lanes), 1)
    own_cell = (lane % (azis * span)) // span * part + lane // (azis * span)
    zero = jnp.zeros((variables, lanes), jnp.float32)
    one = jnp.ones((variables, lanes), jnp.float32)

    def row(j):
        speed = jnp.broadcast_to(
            speeds_ref[j // part][:, j % part : j % part + 1], (variables, lanes)
        )
        return band(speed, visc) + (jnp.where(own_cell == j, 1.0, 0.0),)

    one_back = (zero, zero, zero, zero, -one, zero)
    two_back = (zero, zero, zero, -one, zero, zero)
    rows = []
    for j in range(cells - 2):
        below, above, total, right = row(j)
        lower = below - smooth_implicit * two_back[0]
        upper = above - lower * one_back[1]
        first = -smooth_implicit * two_back[3] - lower * one_back[3]
        second = -smooth_implicit * two_back[4] - lower * one_back[4]
        total = (total - smooth_implicit * two_back[5]) - lower * one_back[5]
        pivot = total - upper - smooth_implicit - first - second
        inverse = 1.0 / pivot
        right = right - smooth_implicit * two_back[2] - lower * one_back[2]
        two_back = one_back
        one_back = (
            upper * inverse,
            smooth_implicit * inverse,
            right * inverse,
            first * inverse,
            second * inverse,
            total * inverse,
        )
        rows.append(one_back)
    after = (zero, zero, -one, zero)
    later = (zero, -one, zero, zero)
    known = [None] * (cells - 2)
    ahead1, ahead2 = (zero, -one, zero, zero), (zero, zero, -one, zero)
    for j in reversed(range(cells - 2)):
        alpha, beta, gamma, first, second, total = rows[j]
        start = (gamma, first, second, total)
        now = tuple(
            (s - beta * far) - alpha * near for s, near, far in zip(start, ahead1, ahead2)
        )
        known[j] = now
        ahead2, ahead1 = ahead1, now
    below, above, total0, right0 = row(cells - 2)
    third, fourth = known[cells - 4], known[cells - 3]
    a01 = above - smooth_implicit * third[2] - below * fourth[2] - smooth_implicit * known[0][2]
    total0 = total0 - smooth_implicit * third[3] - below * fourth[3] - smooth_implicit * known[0][3]
    right0 = right0 - smooth_implicit * third[0] - below * fourth[0] - smooth_implicit * known[0][0]
    below, above, total1, right1 = row(cells - 1)
    a10 = below - smooth_implicit * fourth[1] - above * known[0][1] - smooth_implicit * known[1][1]
    total1 = total1 - smooth_implicit * fourth[3] - above * known[0][3] - smooth_implicit * known[1][3]
    right1 = right1 - smooth_implicit * fourth[0] - above * known[0][0] - smooth_implicit * known[1][0]
    scale = 1.0 / (total0 * total1 - total0 * a10 - total1 * a01)
    value0 = ((total1 - a10) * right0 - a01 * right1) * scale
    value1 = ((total0 - a01) * right1 - a10 * right0) * scale
    values = [k[0] - k[1] * value0 - k[2] * value1 for k in known] + [value0, value1]
    place = lane % span
    for j in range(cells):
        base = (j % part) * azis * span + (j // part) * span
        for l in range(span):
            inverse_ref[pl.ds((base + l) * 8, variables), :] = jnp.where(place == l, values[j], 0.0)


def step_kernel(
    azis,
    walls,
    state_ref,
    speed_azi_ref,
    speed_wall_ref,
    flux_azi_ref,
    flux_wall_ref,
    to_wall_ref,
    mix_char_ref,
    from_azi_ref,
    visc_azi_ref,
    visc_wall_ref,
    out_ref,
    send1,
    recv1,
    send2,
    recv2,
    all_azi,
    all_wall,
    wide,
    alphas,
    betas,
    wall_inv,
    cycle_inv,
    rows_ref,
    blocks,
    fields,
    send1_sem,
    recv1_sem,
    send2_sem,
    recv2_sem,
    azi_send,
    azi_recv,
    wall_send,
    wall_recv,
    own_sem,
):
    variables, part_j, part_k, span_all = state_ref.shape
    count = azis * walls
    span = span_all // count
    lanes = part_j * part_k
    group = azis * span
    wall_cells = walls * part_k
    me_azi = lax.axis_index("azi")
    me_wall = lax.axis_index("wall")
    me = me_azi * walls + me_wall

    barrier = pltpu.get_barrier_semaphore()

    def other(turn):
        target = lax.rem(me + turn, count)
        return target, target // walls, lax.rem(target, walls)

    def greet(turn, _):
        target, azi, wall = other(turn)
        pl.semaphore_signal(barrier, inc=1, device_id=(azi, wall), device_id_type=MESH)
        return 0

    lax.fori_loop(1, count, greet, 0)

    for c in range(variables):
        turned = state_ref[c].reshape(lanes, span_all).T
        for t in range(count):
            send1[c, t] = turned[t * span : (t + 1) * span]

    pl.semaphore_wait(barrier, count - 1)

    def azi_copy(turn):
        azi = lax.rem(me_azi + turn, azis)
        return pltpu.make_async_remote_copy(
            src_ref=speed_azi_ref,
            dst_ref=all_azi.at[me_azi],
            send_sem=azi_send.at[turn],
            recv_sem=azi_recv.at[me_azi],
            device_id=(azi, me_wall),
            device_id_type=MESH,
        )

    def wall_copy(turn):
        wall = lax.rem(me_wall + turn, walls)
        return pltpu.make_async_remote_copy(
            src_ref=speed_wall_ref,
            dst_ref=all_wall.at[me_wall],
            send_sem=wall_send.at[turn],
            recv_sem=wall_recv.at[me_wall],
            device_id=(me_azi, wall),
            device_id_type=MESH,
        )

    def out_copy(turn):
        target, azi, wall = other(turn)
        return pltpu.make_async_remote_copy(
            src_ref=send1.at[:, target],
            dst_ref=recv1.at[me_wall, :, me_azi],
            send_sem=send1_sem.at[turn],
            recv_sem=recv1_sem.at[me],
            device_id=(azi, wall),
            device_id_type=MESH,
        )

    def back_copy(turn):
        target, azi, wall = other(turn)
        return pltpu.make_async_remote_copy(
            src_ref=send2.at[wall, :, azi],
            dst_ref=recv2.at[:, me],
            send_sem=send2_sem.at[turn],
            recv_sem=recv2_sem.at[me],
            device_id=(azi, wall),
            device_id_type=MESH,
        )

    def start_all(make, stop):
        def one(turn, _):
            make(turn).start()
            return 0

        lax.fori_loop(1, stop, one, 0)

    def sent_all(make, stop):
        def one(turn, _):
            make(turn).wait_send()
            return 0

        lax.fori_loop(1, stop, one, 0)

    start_all(wall_copy, walls)
    start_all(azi_copy, azis)
    start_all(out_copy, count)
    own = pltpu.make_async_copy(send1.at[:, me], recv1.at[me_wall, :, me_azi], own_sem.at[0])
    own.start()
    own_azi = pltpu.make_async_copy(speed_azi_ref, all_azi.at[me_azi], own_sem.at[1])
    own_azi.start()
    own_wall = pltpu.make_async_copy(speed_wall_ref, all_wall.at[me_wall], own_sem.at[2])
    own_wall.start()

    def arrived(ref_of, sems, me_index, stop):
        def one(turn, _):
            source = lax.rem(me_index + turn, stop)
            ref = ref_of(source)
            pltpu.make_async_copy(ref, ref, sems.at[source]).wait()
            return 0

        lax.fori_loop(1, stop, one, 0)

    def viscosity(ref):
        index = lax.broadcasted_iota(jnp.int32, (variables, lanes), 0)
        value = jnp.full((variables, lanes), ref[0], jnp.float32)
        for c in range(1, variables):
            value = jnp.where(index == c, ref[c], value)
        return value

    own_wall.wait()
    arrived(lambda w: all_wall.at[w], wall_recv, me_wall, walls)
    wall_inverse(all_wall, viscosity(visc_wall_ref), wide, alphas, betas, wall_inv)
    own_azi.wait()
    arrived(lambda a: all_azi.at[a], azi_recv, me_azi, azis)
    cycle_inverse(all_azi, viscosity(visc_azi_ref), span, cycle_inv)

    own.wait()
    arrived(
        lambda s: recv1.at[lax.rem(s, walls), :, s // walls], recv1_sem, me, count
    )
    lane = lax.broadcasted_iota(jnp.int32, (group, lanes), 1)
    piece = lane // part_k
    for c in range(variables):
        for w in range(walls):
            for a in range(azis):
                rows_ref[c, w, pl.ds(a * span, span), :] = recv1[w, c, a]
    for c in range(variables):
        parts = [rows_ref[c, w] for w in range(walls)]
        for m in range(part_j):
            value = parts[m % walls]
            for w in range(walls):
                moved = parts[w]
                if w != m:
                    moved = pltpu.roll(moved, ((w - m) * part_k) % lanes, 1)
                value = jnp.where(piece == w, moved, value) if w else moved
            blocks[c, m] = value

    def cell(c, m):
        value = blocks[c, m % part_j]
        turns = m // part_j
        return pltpu.roll(value, (-turns * span) % group, 0) if turns else value

    def along(value, by):
        moved = pltpu.roll(value, (-by) % wall_cells, 1)
        keep = lane < wall_cells - by if by > 0 else lane >= -by
        return jnp.where(keep, moved, 0.0)

    for m in range(part_j):
        central_j, central_k, fourth = [], [], []
        for c in range(variables):
            here = cell(c, m)
            up1, up2 = cell(c, m + 1), cell(c, m + 2)
            down1, down2 = cell(c, m - 1), cell(c, m - 2)
            right1, right2 = along(here, 1), along(here, 2)
            left1, left2 = along(here, -1), along(here, -2)
            central_j.append(0.5 * (up1 - down1))
            central_k.append(0.5 * (right1 - left1))
            fourth.append(
                (up2 + down2) + (right2 + left2) - 4.0 * ((up1 + down1) + (right1 + left1)) + 12.0 * here
            )
        flux_j = mix(flux_azi_ref, central_j)
        flux_k = mix(flux_wall_ref, central_k)
        explicit = [
            -time_step * (flux_j[c] + flux_k[c] + smooth_explicit * fourth[c])
            for c in range(variables)
        ]
        turned = mix(to_wall_ref, explicit)
        for c in range(variables):
            fields[c, pl.ds(m * group, group), :] = turned[c]

    for c in range(variables):
        inverse = wall_inv[pl.ds(c, wall_cells, stride=8), :]
        fields[c] = lax.dot_general(
            fields[c],
            inverse,
            (((1,), (1,)), ((), ())),
            precision=highest,
            preferred_element_type=jnp.float32,
        )
    for m in range(part_j):
        rows = pl.ds(m * group, group)
        mixed = mix(mix_char_ref, [fields[c, rows, :] for c in range(variables)])
        for c in range(variables):
            fields[c, rows, :] = mixed[c]
    for c in range(variables):
        inverse = cycle_inv[pl.ds(c, part_j * group, stride=8), :]
        fields[c] = jnp.dot(
            inverse, fields[c], precision=highest, preferred_element_type=jnp.float32
        )
    for m in range(part_j):
        rows = pl.ds(m * group, group)
        mixed = mix(from_azi_ref, [fields[c, rows, :] for c in range(variables)])
        for c in range(variables):
            blocks[c, m] = mixed[c]
    for c in range(variables):
        parts = [blocks[c, m] for m in range(part_j)]
        for w in range(walls):
            value = None
            for m in range(part_j):
                moved = parts[m]
                if w != m:
                    moved = pltpu.roll(moved, ((m - w) * part_k) % lanes, 1)
                value = jnp.where(piece == m, moved, value) if m else moved
            for a in range(azis):
                send2[w, c, a] = value[a * span : (a + 1) * span]

    start_all(back_copy, count)
    own_back = pltpu.make_async_copy(send2.at[me_wall, :, me_azi], recv2.at[:, me], own_sem.at[0])
    own_back.start()
    sent_all(wall_copy, walls)
    sent_all(azi_copy, azis)
    sent_all(out_copy, count)
    own_back.wait()
    arrived(lambda s: recv2.at[:, s], recv2_sem, me, count)
    for c in range(variables):
        for s in range(count):
            fields[c, pl.ds(s * span, span), :] = recv2[c, s]
    for c in range(variables):
        out_ref[c] = fields[c].T.reshape(part_j, part_k, span_all)
    sent_all(back_copy, count)


def per_device_whole_lines(
    state,
    flux_azi,
    flux_wall,
    to_wall,
    mix_char,
    from_azi,
    speed_azi,
    speed_wall,
    visc_azi,
    visc_wall,
):
    azis, walls = lax.axis_size("azi"), lax.axis_size("wall")
    count = azis * walls
    variables, part_j, part_k, span_all = state.shape
    span = span_all // count
    lanes = part_j * part_k
    wall_cells = walls * part_k
    vmem = pl.BlockSpec(memory_space=pltpu.VMEM)
    smem = pl.BlockSpec(memory_space=pltpu.SMEM)
    f32 = jnp.float32
    dma = pltpu.SemaphoreType.DMA
    return pl.pallas_call(
        functools.partial(step_kernel, azis, walls),
        out_shape=jax.ShapeDtypeStruct(state.shape, f32),
        in_specs=[vmem] * 3 + [smem] * 7,
        out_specs=vmem,
        scratch_shapes=[
            pltpu.VMEM((variables, count, span, lanes), f32),
            pltpu.VMEM((walls, variables, azis, span, lanes), f32),
            pltpu.VMEM((walls, variables, azis, span, lanes), f32),
            pltpu.VMEM((variables, count, span, lanes), f32),
            pltpu.VMEM((azis,) + speed_azi.shape, f32),
            pltpu.VMEM((walls,) + speed_wall.shape, f32),
            pltpu.VMEM((wall_cells, variables, lanes), f32),
            pltpu.VMEM((wall_cells, variables, lanes), f32),
            pltpu.VMEM((wall_cells, variables, lanes), f32),
            pltpu.VMEM((wall_cells * 8, lanes), f32),
            pltpu.VMEM((part_j * azis * span * 8, lanes), f32),
            pltpu.VMEM((variables, walls, azis * span, lanes), f32),
            pltpu.VMEM((variables, part_j, azis * span, lanes), f32),
            pltpu.VMEM((variables, span_all, lanes), f32),
            dma((count,)),
            dma((count,)),
            dma((count,)),
            dma((count,)),
            dma((azis,)),
            dma((azis,)),
            dma((walls,)),
            dma((walls,)),
            dma((3,)),
        ],
        compiler_params=pltpu.CompilerParams(collective_id=0, has_side_effects=True),
    )(
        state,
        speed_azi,
        speed_wall,
        flux_azi,
        flux_wall,
        to_wall,
        mix_char,
        from_azi,
        visc_azi,
        visc_wall,
    )


def whole_lines_fit(mesh, variables, part_j, part_k, span_all):
    azis, walls = mesh.shape["azi"], mesh.shape["wall"]
    count = azis * walls
    lanes = part_j * part_k
    return (
        span_all % count == 0
        and lanes == 128
        and span_all == lanes
        and walls * part_k == lanes
        and walls == part_j
        and azis * (span_all // count) * part_j == lanes
        and (azis * (span_all // count)) % 8 == 0
        and azis * part_j >= 8
        and variables <= 8
    )


def solution(mesh):
    in_specs = (
        P(None, "azi", "wall", None),
        P(),
        P(),
        P(),
        P(),
        P(),
        P(None, "azi"),
        P(None, "wall"),
        P(),
        P(),
    )
    out_specs = P(None, "azi", "wall", None)

    def chosen(state, *rest):
        if whole_lines_fit(mesh, *state.shape):
            return per_device_whole_lines(state, *rest)
        return per_device(state, *rest)

    return jax.shard_map(
        chosen, mesh=mesh, in_specs=in_specs, out_specs=out_specs, check_vma=False
    )
```

```python
import functools

import jax
import jax.numpy as jnp
from jax import lax
from jax.experimental import pallas as pl
from jax.experimental.pallas import tpu as pltpu
from jax.sharding import PartitionSpec as P

time_step = 4096.0
smooth_explicit = 0.02
smooth_implicit = 0.04
highest = lax.Precision.HIGHEST


def padded(value, sides, width, wrap):
    for axis, dim in sides:
        size, length = (lax.axis_size(axis), value.shape[dim])
        up = [(i, (i + 1) % size) for i in range(size if wrap else size - 1)]
        down = [(j, i) for i, j in up]
        last = lax.slice_in_dim(value, length - width, length, axis=dim)
        initial = lax.slice_in_dim(value, 0, width, axis=dim)
        before = lax.ppermute(last, axis, up)
        after = lax.ppermute(initial, axis, down)
        value = jnp.concatenate([before, value, after], axis=dim)
    return value


def from_behind(value, axis, by):
    size = lax.axis_size(axis)
    pairs = [(i, i + by) for i in range(size) if 0 <= i + by < size]
    return lax.ppermute(value, axis, pairs)


def from_behind_2(block, axis, distance):
    devices = range(lax.axis_size(axis))
    route = [((i - distance) % len(devices), i) for i in devices]
    return lax.ppermute(block, axis, route)


def mixing(matrix, field):
    return jnp.einsum("ab,bjkl->ajkl", matrix, field, precision=highest)


def residual(padded_azi, padded_wall, flux_azi, flux_wall):
    azi_flux = mixing(flux_azi, padded_azi[:, 1:-1])
    wall_flux = mixing(flux_wall, padded_wall[:, :, 1:-1])
    central = 0.5 * (azi_flux[:, 2:] - azi_flux[:, :-2]) + 0.5 * (
        wall_flux[:, :, 2:] - wall_flux[:, :, :-2]
    )
    fourth = (
        padded_azi[:, 4:]
        - 4.0 * padded_azi[:, 3:-1]
        + 6.0 * padded_azi[:, 2:-2]
        - 4.0 * padded_azi[:, 1:-3]
        + padded_azi[:, :-4]
    )
    fourth = (
        fourth
        + padded_wall[:, :, 4:]
        - 4.0 * padded_wall[:, :, 3:-1]
        + 6.0 * padded_wall[:, :, 2:-2]
        - 4.0 * padded_wall[:, :, 1:-3]
        + padded_wall[:, :, :-4]
    )
    return -time_step * (central + smooth_explicit * fourth)


def coefficients(speed, visc):
    viscous = visc[:, None]
    below = -0.5 * time_step * speed - viscous - 4.0 * smooth_implicit
    above = 0.5 * time_step * speed - viscous - 4.0 * smooth_implicit
    centre = 1.0 + 2.0 * viscous + 6.0 * smooth_implicit
    return (below, above, centre)


def invert(matrices):
    extent = matrices.shape[-1]
    last_axis = matrices.ndim - 1
    identity = jnp.broadcast_to(jnp.eye(extent, dtype=matrices.dtype), matrices.shape)
    marks = lax.broadcasted_iota(jnp.int32, (extent, 1), 0)

    def eliminate(turn, running):
        working, inverse = running
        pivot_row = lax.dynamic_index_in_dim(working, turn, last_axis - 1, keepdims=False)
        inverse_row = lax.dynamic_index_in_dim(inverse, turn, last_axis - 1, keepdims=False)
        column = lax.dynamic_index_in_dim(working, turn, last_axis, keepdims=True)
        pivot = lax.dynamic_index_in_dim(pivot_row, turn, last_axis - 1, keepdims=True)
        pivot_row = pivot_row / pivot
        inverse_row = inverse_row / pivot
        working = working - column * pivot_row[..., None, :]
        inverse = inverse - column * inverse_row[..., None, :]
        on_row = marks == turn
        working = jnp.where(on_row, pivot_row[..., None, :], working)
        inverse = jnp.where(on_row, inverse_row[..., None, :], inverse)
        return (working, inverse)

    return lax.fori_loop(0, extent, eliminate, (matrices, identity))[1]


def two_by_two(first, second, third, fourth):
    return jnp.stack([jnp.stack([first, second], -1), jnp.stack([third, fourth], -1)], -2)


def invert_two(blocks):
    first = blocks[..., 0, 0]
    second = blocks[..., 0, 1]
    third = blocks[..., 1, 0]
    fourth = blocks[..., 1, 1]
    determinant = first * fourth - second * third
    return two_by_two(
        fourth / determinant, -second / determinant, -third / determinant, first / determinant
    )


def block_product(first, second):
    return jnp.einsum("cmab,cmbd->cmad", first, second, precision=highest)


def block_apply(blocks, field):
    return jnp.einsum("cmab,cmbkl->cmakl", blocks, field, precision=highest)


def apply_four(matrix, field):
    return jnp.einsum("cqr,cjrl->cjql", matrix, field, precision=highest)


def product_four(first, second):
    return jnp.einsum("cab,cbd->cad", first, second, precision=highest)


def cyclic_levels(speeds, visc):
    below, above, centre = coefficients(speeds, visc)
    below_even = below[:, 0::2]
    below_odd = below[:, 1::2]
    above_even = above[:, 0::2]
    above_odd = above[:, 1::2]
    edge_value = jnp.full_like(below_even, smooth_implicit)
    nought = jnp.zeros_like(below_even)
    middle_diag = jnp.broadcast_to(centre, below_even.shape)
    behind_block = two_by_two(edge_value, below_even, nought, edge_value)
    middle = two_by_two(middle_diag, above_even, below_odd, middle_diag)
    ahead_block = two_by_two(edge_value, nought, above_odd, edge_value)
    blocks = below_even.shape[1]
    stride = 1
    levels = []
    while stride < blocks:
        weight_before = -block_product(behind_block, invert_two(jnp.roll(middle, stride, 1)))
        weight_after = -block_product(ahead_block, invert_two(jnp.roll(middle, -stride, 1)))
        middle = (
            middle
            + block_product(weight_before, jnp.roll(ahead_block, stride, 1))
            + block_product(weight_after, jnp.roll(behind_block, -stride, 1))
        )
        behind_block = block_product(weight_before, jnp.roll(behind_block, stride, 1))
        ahead_block = block_product(weight_after, jnp.roll(ahead_block, -stride, 1))
        levels.append((stride, weight_before, weight_after))
        stride = stride * 2
    return (levels, invert_two(behind_block + middle + ahead_block))


def per_device(
    state,
    flux_azi,
    flux_wall,
    to_wall,
    mix_char,
    from_azi,
    speed_azi,
    speed_wall,
    visc_azi,
    visc_wall,
):
    padded_azi = padded(state, (("azi", 1),), 2, True)
    padded_wall = padded(state, (("wall", 2),), 2, False)
    explicit = residual(padded_azi, padded_wall, flux_azi, flux_wall)
    char_wall = mixing(to_wall, explicit)
    variables = state.shape[0]
    cycle_cells = state.shape[1]
    wall_depth = state.shape[2]
    span_cells = state.shape[3]
    below, above, centre = coefficients(speed_wall, visc_wall)

    def shifted(offset):
        return jnp.eye(wall_depth, k=offset, dtype=jnp.float32)

    wall_band = (
        centre[:, :, None] * shifted(0)
        + below[:, :, None] * shifted(-1)
        + above[:, :, None] * shifted(1)
        + smooth_implicit * (shifted(2) + shifted(-2))
    )
    local_inverse = invert(wall_band)
    solved = jnp.einsum("ckm,cjml->cjkl", local_inverse, char_wall, precision=highest)
    edge_value = jnp.full_like(below[:, 0], smooth_implicit)
    nought = jnp.zeros_like(edge_value)
    spike_low = jnp.einsum(
        "cka,cab->ckb",
        local_inverse[:, :, 0:2],
        two_by_two(edge_value, below[:, 0], nought, edge_value),
        precision=highest,
    )
    spike_high = jnp.einsum(
        "cka,cab->ckb",
        local_inverse[:, :, wall_depth - 2 :],
        two_by_two(edge_value, nought, above[:, wall_depth - 1], edge_value),
        precision=highest,
    )
    padding = jnp.zeros((variables, 4, 2), jnp.float32)
    ends_low = jnp.concatenate([spike_low[:, 0:2], spike_low[:, wall_depth - 2 :]], 1)
    ends_high = jnp.concatenate([spike_high[:, 0:2], spike_high[:, wall_depth - 2 :]], 1)
    coupling_prev = jnp.concatenate([padding, ends_low], 2)
    coupling_next = jnp.concatenate([ends_high, padding], 2)
    interface = jnp.concatenate([solved[:, :, 0:2], solved[:, :, wall_depth - 2 :]], 2)
    wall_place = lax.axis_index("wall")
    wall_count = lax.axis_size("wall")
    every_prev, every_next = (
        lax.all_gather(coupling_prev, "wall", axis=1, tiled=True),
        lax.all_gather(coupling_next, "wall", axis=1, tiled=True),
    )
    carried = jnp.zeros((variables, 4, 4), jnp.float32)
    identity = jnp.broadcast_to(jnp.eye(4, dtype=jnp.float32), (variables, 4, 4))
    inverses = []
    forwards = []
    for member in range(wall_count):
        pivot_block = identity - product_four(every_prev[:, 4 * member : 4 * member + 4], carried)
        pivot_inverse = invert(pivot_block)
        carried = product_four(pivot_inverse, every_next[:, 4 * member : 4 * member + 4])
        inverses.append(pivot_inverse)
        forwards.append(carried)
    own_inverse = lax.dynamic_index_in_dim(jnp.stack(inverses), wall_place, 0, keepdims=False)
    own_forward = lax.dynamic_index_in_dim(jnp.stack(forwards), wall_place, 0, keepdims=False)
    partial_values = jnp.zeros_like(interface)
    for turn in range(wall_count):
        arrived = from_behind(partial_values, "wall", 1)
        fresh = apply_four(own_inverse, interface - apply_four(coupling_prev, arrived))
        partial_values = jnp.where(wall_place == turn, fresh, partial_values)
    end_values = jnp.zeros_like(interface)
    ahead = jnp.zeros((variables, cycle_cells, 2, span_cells), jnp.float32)
    for turn in reversed(range(wall_count)):
        arrived = from_behind(end_values, "wall", -1)
        fresh = partial_values - apply_four(own_forward, arrived)
        end_values = jnp.where(wall_place == turn, fresh, end_values)
        ahead = jnp.where(wall_place == turn, arrived[:, :, 0:2], ahead)
    behind = from_behind(end_values, "wall", 1)[:, :, 2:4]
    wall_result = (
        solved
        - jnp.einsum("cka,cjal->cjkl", spike_low, behind, precision=highest)
        - jnp.einsum("cka,cjal->cjkl", spike_high, ahead, precision=highest)
    )
    cycle_input = mixing(mix_char, wall_result)
    speeds = lax.all_gather(speed_azi, "azi", axis=1, tiled=True)
    levels, closing = cyclic_levels(speeds, visc_azi)
    half_cells = cycle_cells // 2
    cycle_place = lax.axis_index("azi")

    def own_rows(blocks):
        return lax.dynamic_slice_in_dim(blocks, cycle_place * half_cells, half_cells, 1)

    right_side = cycle_input.reshape(variables, half_cells, 2, wall_depth, span_cells)
    for stride, weight_before, weight_after in levels:
        device_hop = max(1, stride // half_cells)
        reach = min(stride, half_cells)
        from_before = from_behind_2(right_side[:, half_cells - reach :], "azi", device_hop)
        from_after = from_behind_2(right_side[:, :reach], "azi", -device_hop)
        rows_minus = jnp.concatenate([from_before, right_side[:, : half_cells - reach]], 1)
        rows_plus = jnp.concatenate([right_side[:, reach:], from_after], 1)
        right_side = (
            right_side
            + block_apply(own_rows(weight_before), rows_minus)
            + block_apply(own_rows(weight_after), rows_plus)
        )
    cycle_result = block_apply(own_rows(closing), right_side).reshape(
        variables, cycle_cells, wall_depth, span_cells
    )
    return mixing(from_azi, cycle_result)


MESH = pl.DeviceIdType.MESH


def band(speed, visc):
    below = -0.5 * time_step * speed - visc - 4.0 * smooth_implicit
    above = 0.5 * time_step * speed - visc - 4.0 * smooth_implicit
    centre = 1.0 + 2.0 * visc + 6.0 * smooth_implicit
    both = below + above
    part = both - below
    lost = (below - (both - part)) + (above - part)
    total = (centre + both) + lost + 2.0 * smooth_implicit
    return below, above, total


def mix(matrix_ref, fields):
    result = []
    for a in range(len(fields)):
        value = matrix_ref[a, 0] * fields[0]
        for b in range(1, len(fields)):
            value = value + matrix_ref[a, b] * fields[b]
        result.append(value)
    return result


def wall_inverse(speeds_ref, visc, wide_ref, alpha_ref, beta_ref, inverse_ref):
    walls, variables, part = speeds_ref.shape
    cells = walls * part
    lanes = wide_ref.shape[-1]
    for w in range(walls):
        block = speeds_ref[w]
        for k in range(part):
            wide_ref[w * part + k] = jnp.broadcast_to(block[:, k : k + 1], (variables, lanes))
    lane = lax.broadcasted_iota(jnp.int32, (variables, lanes), 1)
    both = lane + lax.broadcasted_iota(jnp.int32, (variables, lanes), 0)
    zero = jnp.where(both < 0, 1.0, 0.0)
    one = jnp.where(both < 0, 0.0, 1.0)

    def forward(k, carry):
        alpha1, beta1, gamma1, sum1, alpha2, beta2, gamma2, sum2 = carry
        below, above, total = band(wide_ref[k], visc)
        lower = below - smooth_implicit * alpha2
        upper = above - lower * beta1
        total = (total - smooth_implicit * sum2) - lower * sum1
        pivot = total - upper - smooth_implicit
        inverse = 1.0 / pivot
        right = jnp.where(lane == k, 1.0, 0.0) - smooth_implicit * gamma2 - lower * gamma1
        alpha = upper * inverse
        beta = smooth_implicit * inverse
        gamma = right * inverse
        alpha_ref[k] = alpha
        beta_ref[k] = beta
        inverse_ref[pl.ds(pl.multiple_of(k * 8, 8), variables), :] = gamma
        return (alpha, beta, gamma, total * inverse, alpha1, beta1, gamma1, sum1)

    lax.fori_loop(0, cells, forward, (zero, zero, zero, one, zero, zero, zero, one), unroll=2)

    def backward(turn, carry):
        x1, x2 = carry
        k = cells - 1 - turn
        rows = pl.ds(pl.multiple_of(k * 8, 8), variables)
        x = (inverse_ref[rows, :] - beta_ref[k] * x2) - alpha_ref[k] * x1
        inverse_ref[rows, :] = x
        return (x, x1)

    lax.fori_loop(0, cells, backward, (zero, zero), unroll=2)


def cycle_inverse(speeds_ref, visc, span, inverse_ref):
    azis, part, variables = speeds_ref.shape
    cells = azis * part
    lanes = inverse_ref.shape[-1]
    lane = lax.broadcasted_iota(jnp.int32, (variables, lanes), 1)
    own_cell = (lane % (azis * span)) // span * part + lane // (azis * span)
    zero = jnp.zeros((variables, lanes), jnp.float32)
    one = jnp.ones((variables, lanes), jnp.float32)

    speeds = [speeds_ref[a].T for a in range(azis)]

    def row(j):
        speed = jnp.broadcast_to(
            speeds[j // part][:, j % part : j % part + 1], (variables, lanes)
        )
        return band(speed, visc) + (jnp.where(own_cell == j, 1.0, 0.0),)

    one_back = (zero, zero, zero, zero, -one, zero)
    two_back = (zero, zero, zero, -one, zero, zero)
    rows = []
    for j in range(cells - 2):
        below, above, total, right = row(j)
        lower = below - smooth_implicit * two_back[0]
        upper = above - lower * one_back[1]
        first = -smooth_implicit * two_back[3] - lower * one_back[3]
        second = -smooth_implicit * two_back[4] - lower * one_back[4]
        total = (total - smooth_implicit * two_back[5]) - lower * one_back[5]
        pivot = total - upper - smooth_implicit - first - second
        inverse = 1.0 / pivot
        right = right - smooth_implicit * two_back[2] - lower * one_back[2]
        two_back = one_back
        one_back = (
            upper * inverse,
            smooth_implicit * inverse,
            right * inverse,
            first * inverse,
            second * inverse,
            total * inverse,
        )
        rows.append(one_back)
    after = (zero, zero, -one, zero)
    later = (zero, -one, zero, zero)
    known = [None] * (cells - 2)
    ahead1, ahead2 = (zero, -one, zero, zero), (zero, zero, -one, zero)
    for j in reversed(range(cells - 2)):
        alpha, beta, gamma, first, second, total = rows[j]
        start = (gamma, first, second, total)
        now = tuple(
            (s - beta * far) - alpha * near for s, near, far in zip(start, ahead1, ahead2)
        )
        known[j] = now
        ahead2, ahead1 = ahead1, now
    below, above, total0, right0 = row(cells - 2)
    third, fourth = known[cells - 4], known[cells - 3]
    a01 = above - smooth_implicit * third[2] - below * fourth[2] - smooth_implicit * known[0][2]
    total0 = total0 - smooth_implicit * third[3] - below * fourth[3] - smooth_implicit * known[0][3]
    right0 = right0 - smooth_implicit * third[0] - below * fourth[0] - smooth_implicit * known[0][0]
    below, above, total1, right1 = row(cells - 1)
    a10 = below - smooth_implicit * fourth[1] - above * known[0][1] - smooth_implicit * known[1][1]
    total1 = total1 - smooth_implicit * fourth[3] - above * known[0][3] - smooth_implicit * known[1][3]
    right1 = right1 - smooth_implicit * fourth[0] - above * known[0][0] - smooth_implicit * known[1][0]
    scale = 1.0 / (total0 * total1 - total0 * a10 - total1 * a01)
    value0 = ((total1 - a10) * right0 - a01 * right1) * scale
    value1 = ((total0 - a01) * right1 - a10 * right0) * scale
    values = [k[0] - k[1] * value0 - k[2] * value1 for k in known] + [value0, value1]
    place = lane % span
    for j in range(cells):
        base = (j % part) * azis * span + (j // part) * span
        for l in range(span):
            inverse_ref[pl.ds((base + l) * 8, variables), :] = jnp.where(place == l, values[j], 0.0)


def step_kernel(
    azis,
    walls,
    state_hbm,
    speed_azi_hbm,
    speed_wall_hbm,
    flux_azi_hbm,
    flux_wall_hbm,
    to_wall_hbm,
    mix_char_hbm,
    from_azi_hbm,
    visc_azi_hbm,
    visc_wall_hbm,
    out_ref,
    send1,
    recv1,
    send2,
    recv2,
    all_azi,
    all_wall,
    wide,
    alphas,
    betas,
    wall_inv,
    cycle_inv,
    rows_ref,
    blocks,
    fields,
    send1_sem,
    recv1_sem,
    send2_sem,
    recv2_sem,
    azi_send,
    azi_recv,
    wall_send,
    wall_recv,
    own_sem,
    in_sem,
    state_ref,
    speed_azi_ref,
    speed_wall_ref,
    flux_azi_ref,
    flux_wall_ref,
    to_wall_ref,
    mix_char_ref,
    from_azi_ref,
    visc_azi_ref,
    visc_wall_ref,
):
    variables, part_j, part_k, span_all = state_hbm.shape
    count = azis * walls
    span = span_all // count
    lanes = part_j * part_k
    group = azis * span
    wall_cells = walls * part_k
    me_azi = lax.axis_index("azi")
    me_wall = lax.axis_index("wall")
    me = me_azi * walls + me_wall

    barrier = pltpu.get_barrier_semaphore()

    def other(turn):
        target = lax.rem(me + turn, count)
        return target, target // walls, lax.rem(target, walls)

    def greet(turn, _):
        target, azi, wall = other(turn)
        pl.semaphore_signal(barrier, inc=1, device_id=(azi, wall), device_id_type=MESH)
        return 0

    lax.fori_loop(1, count, greet, 0)

    whole = (
        (state_hbm, state_ref),
        (speed_azi_hbm, speed_azi_ref),
        (speed_wall_hbm, speed_wall_ref),
        (flux_azi_hbm, flux_azi_ref),
        (flux_wall_hbm, flux_wall_ref),
        (to_wall_hbm, to_wall_ref),
        (mix_char_hbm, mix_char_ref),
        (from_azi_hbm, from_azi_ref),
        (visc_azi_hbm, visc_azi_ref),
        (visc_wall_hbm, visc_wall_ref),
    )
    taken = [
        pltpu.make_async_copy(there, here, in_sem.at[i]) for i, (there, here) in enumerate(whole)
    ]
    for copy in taken:
        copy.start()
    taken[0].wait()

    for c in range(variables):
        turned = state_ref[c].reshape(lanes, span_all).T
        for t in range(count):
            send1[t, c] = turned[t * span : (t + 1) * span]

    for copy in taken[1:]:
        copy.wait()
    pl.semaphore_wait(barrier, count - 1)

    def azi_copy(turn):
        azi = lax.rem(me_azi + turn, azis)
        return pltpu.make_async_remote_copy(
            src_ref=speed_azi_ref,
            dst_ref=all_azi.at[me_azi],
            send_sem=azi_send.at[turn],
            recv_sem=azi_recv.at[me_azi],
            device_id=(azi, me_wall),
            device_id_type=MESH,
        )

    def wall_copy(turn):
        wall = lax.rem(me_wall + turn, walls)
        return pltpu.make_async_remote_copy(
            src_ref=speed_wall_ref,
            dst_ref=all_wall.at[me_wall],
            send_sem=wall_send.at[turn],
            recv_sem=wall_recv.at[me_wall],
            device_id=(me_azi, wall),
            device_id_type=MESH,
        )

    def out_copy(turn):
        target, azi, wall = other(turn)
        return pltpu.make_async_remote_copy(
            src_ref=send1.at[target],
            dst_ref=recv1.at[me],
            send_sem=send1_sem.at[turn],
            recv_sem=recv1_sem.at[me],
            device_id=(azi, wall),
            device_id_type=MESH,
        )

    def back_copy(turn):
        target, azi, wall = other(turn)
        return pltpu.make_async_remote_copy(
            src_ref=send2.at[target],
            dst_ref=recv2.at[me],
            send_sem=send2_sem.at[turn],
            recv_sem=recv2_sem.at[me],
            device_id=(azi, wall),
            device_id_type=MESH,
        )

    def start_all(make, stop):
        def one(turn, _):
            make(turn).start()
            return 0

        lax.fori_loop(1, stop, one, 0)

    def sent_all(make, stop):
        def one(turn, _):
            make(turn).wait_send()
            return 0

        lax.fori_loop(1, stop, one, 0)

    start_all(wall_copy, walls)
    start_all(azi_copy, azis)
    start_all(out_copy, count)
    own = pltpu.make_async_copy(send1.at[me], recv1.at[me], own_sem.at[0])
    own.start()
    own_azi = pltpu.make_async_copy(speed_azi_ref, all_azi.at[me_azi], own_sem.at[1])
    own_azi.start()
    own_wall = pltpu.make_async_copy(speed_wall_ref, all_wall.at[me_wall], own_sem.at[2])
    own_wall.start()

    def arrived(ref_of, sems, me_index, stop):
        def one(turn, _):
            source = lax.rem(me_index + turn, stop)
            ref = ref_of(source)
            pltpu.make_async_copy(ref, ref, sems.at[source]).wait()
            return 0

        lax.fori_loop(1, stop, one, 0)

    def viscosity(ref):
        index = lax.broadcasted_iota(jnp.int32, (variables, lanes), 0)
        value = jnp.full((variables, lanes), ref[0], jnp.float32)
        for c in range(1, variables):
            value = jnp.where(index == c, ref[c], value)
        return value

    own_wall.wait()
    arrived(lambda w: all_wall.at[w], wall_recv, me_wall, walls)
    wall_inverse(all_wall, viscosity(visc_wall_ref), wide, alphas, betas, wall_inv)
    own_azi.wait()
    arrived(lambda a: all_azi.at[a], azi_recv, me_azi, azis)
    cycle_inverse(all_azi, viscosity(visc_azi_ref), span, cycle_inv)

    own.wait()
    arrived(lambda s: recv1.at[s], recv1_sem, me, count)
    lane = lax.broadcasted_iota(jnp.int32, (group, lanes), 1)
    piece = lane // part_k
    for c in range(variables):
        for w in range(walls):
            for a in range(azis):
                rows_ref[c, w, pl.ds(a * span, span), :] = recv1[a * walls + w, c]
    for c in range(variables):
        parts = [rows_ref[c, w] for w in range(walls)]
        for m in range(part_j):
            value = parts[m % walls]
            for w in range(walls):
                moved = parts[w]
                if w != m:
                    moved = pltpu.roll(moved, ((w - m) * part_k) % lanes, 1)
                value = jnp.where(piece == w, moved, value) if w else moved
            blocks[c, m] = value

    def cell(c, m):
        value = blocks[c, m % part_j]
        turns = m // part_j
        return pltpu.roll(value, (-turns * span) % group, 0) if turns else value

    def along(value, by):
        moved = pltpu.roll(value, (-by) % wall_cells, 1)
        keep = lane < wall_cells - by if by > 0 else lane >= -by
        return jnp.where(keep, moved, 0.0)

    for m in range(part_j):
        central_j, central_k, fourth = [], [], []
        for c in range(variables):
            here = cell(c, m)
            up1, up2 = cell(c, m + 1), cell(c, m + 2)
            down1, down2 = cell(c, m - 1), cell(c, m - 2)
            right1, right2 = along(here, 1), along(here, 2)
            left1, left2 = along(here, -1), along(here, -2)
            central_j.append(0.5 * (up1 - down1))
            central_k.append(0.5 * (right1 - left1))
            fourth.append(
                (up2 + down2) + (right2 + left2) - 4.0 * ((up1 + down1) + (right1 + left1)) + 12.0 * here
            )
        flux_j = mix(flux_azi_ref, central_j)
        flux_k = mix(flux_wall_ref, central_k)
        explicit = [
            -time_step * (flux_j[c] + flux_k[c] + smooth_explicit * fourth[c])
            for c in range(variables)
        ]
        turned = mix(to_wall_ref, explicit)
        for c in range(variables):
            fields[c, pl.ds(m * group, group), :] = turned[c]

    for c in range(variables):
        inverse = wall_inv[pl.ds(c, wall_cells, stride=8), :]
        fields[c] = lax.dot_general(
            fields[c],
            inverse,
            (((1,), (1,)), ((), ())),
            precision=highest,
            preferred_element_type=jnp.float32,
        )
    for m in range(part_j):
        rows = pl.ds(m * group, group)
        mixed = mix(mix_char_ref, [fields[c, rows, :] for c in range(variables)])
        for c in range(variables):
            fields[c, rows, :] = mixed[c]
    for c in range(variables):
        inverse = cycle_inv[pl.ds(c, part_j * group, stride=8), :]
        fields[c] = jnp.dot(
            inverse, fields[c], precision=highest, preferred_element_type=jnp.float32
        )
    for m in range(part_j):
        rows = pl.ds(m * group, group)
        mixed = mix(from_azi_ref, [fields[c, rows, :] for c in range(variables)])
        for c in range(variables):
            blocks[c, m] = mixed[c]
    for c in range(variables):
        parts = [blocks[c, m] for m in range(part_j)]
        for w in range(walls):
            value = None
            for m in range(part_j):
                moved = parts[m]
                if w != m:
                    moved = pltpu.roll(moved, ((m - w) * part_k) % lanes, 1)
                value = jnp.where(piece == m, moved, value) if m else moved
            for a in range(azis):
                send2[a * walls + w, c] = value[a * span : (a + 1) * span]

    start_all(back_copy, count)
    own_back = pltpu.make_async_copy(send2.at[me], recv2.at[me], own_sem.at[0])
    own_back.start()
    sent_all(wall_copy, walls)
    sent_all(azi_copy, azis)
    sent_all(out_copy, count)
    own_back.wait()
    arrived(lambda s: recv2.at[s], recv2_sem, me, count)
    for c in range(variables):
        for s in range(count):
            fields[c, pl.ds(s * span, span), :] = recv2[s, c]
    given = []
    for c in range(variables):
        state_ref[c] = fields[c].T.reshape(part_j, part_k, span_all)
        copy = pltpu.make_async_copy(state_ref.at[c], out_ref.at[c], in_sem.at[c])
        copy.start()
        given.append(copy)
    for copy in given:
        copy.wait()
    sent_all(back_copy, count)


def per_device_whole_lines(
    state,
    flux_azi,
    flux_wall,
    to_wall,
    mix_char,
    from_azi,
    speed_azi,
    speed_wall,
    visc_azi,
    visc_wall,
):
    azis, walls = lax.axis_size("azi"), lax.axis_size("wall")
    count = azis * walls
    variables, part_j, part_k, span_all = state.shape
    span = span_all // count
    lanes = part_j * part_k
    wall_cells = walls * part_k
    f32 = jnp.float32
    dma = pltpu.SemaphoreType.DMA
    return pl.pallas_call(
        functools.partial(step_kernel, azis, walls),
        out_shape=jax.ShapeDtypeStruct(state.shape, f32),
        in_specs=[pl.BlockSpec(memory_space=pl.ANY)] * 10,
        out_specs=pl.BlockSpec(memory_space=pl.ANY),
        scratch_shapes=[
            pltpu.VMEM((count, variables, span, lanes), f32),
            pltpu.VMEM((count, variables, span, lanes), f32),
            pltpu.VMEM((count, variables, span, lanes), f32),
            pltpu.VMEM((count, variables, span, lanes), f32),
            pltpu.VMEM((azis,) + speed_azi.shape[::-1], f32),
            pltpu.VMEM((walls,) + speed_wall.shape, f32),
            pltpu.VMEM((wall_cells, variables, lanes), f32),
            pltpu.VMEM((wall_cells, variables, lanes), f32),
            pltpu.VMEM((wall_cells, variables, lanes), f32),
            pltpu.VMEM((wall_cells * 8, lanes), f32),
            pltpu.VMEM((part_j * azis * span * 8, lanes), f32),
            pltpu.VMEM((variables, walls, azis * span, lanes), f32),
            pltpu.VMEM((variables, part_j, azis * span, lanes), f32),
            pltpu.VMEM((variables, span_all, lanes), f32),
            dma((count,)),
            dma((count,)),
            dma((count,)),
            dma((count,)),
            dma((azis,)),
            dma((azis,)),
            dma((walls,)),
            dma((walls,)),
            dma((3,)),
            dma((10,)),
            pltpu.VMEM(state.shape, f32),
            pltpu.VMEM(speed_azi.shape[::-1], f32),
            pltpu.VMEM(speed_wall.shape, f32),
            pltpu.SMEM(flux_azi.shape, f32),
            pltpu.SMEM(flux_wall.shape, f32),
            pltpu.SMEM(to_wall.shape, f32),
            pltpu.SMEM(mix_char.shape, f32),
            pltpu.SMEM(from_azi.shape, f32),
            pltpu.SMEM(visc_azi.shape, f32),
            pltpu.SMEM(visc_wall.shape, f32),
        ],
        compiler_params=pltpu.CompilerParams(collective_id=0, has_side_effects=True),
    )(
        state,
        speed_azi.T,
        speed_wall,
        flux_azi,
        flux_wall,
        to_wall,
        mix_char,
        from_azi,
        visc_azi,
        visc_wall,
    )


def whole_lines_fit(mesh, variables, part_j, part_k, span_all):
    azis, walls = mesh.shape["azi"], mesh.shape["wall"]
    count = azis * walls
    lanes = part_j * part_k
    return (
        span_all % count == 0
        and lanes == 128
        and span_all == lanes
        and walls * part_k == lanes
        and walls == part_j
        and azis * (span_all // count) * part_j == lanes
        and (azis * (span_all // count)) % 8 == 0
        and azis * part_j >= 8
        and variables <= 8
    )


def solution(mesh):
    in_specs = (
        P(None, "azi", "wall", None),
        P(),
        P(),
        P(),
        P(),
        P(),
        P(None, "azi"),
        P(None, "wall"),
        P(),
        P(),
    )
    out_specs = P(None, "azi", "wall", None)

    def chosen(state, *rest):
        if whole_lines_fit(mesh, *state.shape):
            return per_device_whole_lines(state, *rest)
        return per_device(state, *rest)

    return jax.shard_map(
        chosen, mesh=mesh, in_specs=in_specs, out_specs=out_specs, check_vma=False
    )
```
